32 devices in a mesh: dp: 4 (over y, x), row: 8 (over z, core).
Axes of the slice: x: 2, y: 2, z: 4, core: 2. Of those that a mesh axis runs over, the one named last changes fastest.
Arguments:
- bag_index: int32 [16384, 16], P(('dp', 'row')), may hold values from 0 to 4223, as said below
- pooled_grad: bfloat16 [16384, 256], P(('dp', 'row')), may hold values from -6 to 6
- touched_ids: int32 [32, 128], P(('dp', 'row')), may hold values from 0 to 1023, as said below
- owner_counts: int32 [32, 32], P(('dp', 'row')), may hold values from 1 to 8, as said below
- cold_table: float32 [32768, 256], P(('dp', 'row')), may hold values from -6 to 6
- cold_moment_codes: bfloat16 [32768, 256], P(('dp', 'row')), may hold values from -1 to 1
- cold_second_codes: bfloat16 [32768, 256], P(('dp', 'row')), may hold values from 0.049804688 to 1
- cold_moment_scales: float32 [32768], P(('dp', 'row')), may hold values from 0.05 to 2
- cold_second_scales: float32 [32768], P(('dp', 'row')), may hold values from 0.01 to 1
- hot_table: float32 [4096, 256], replicated, may hold values from -6 to 6
- hot_moment_codes: bfloat16 [4096, 256], P('row'), may hold values from -1 to 1
- hot_second_codes: bfloat16 [4096, 256], P('row'), may hold values from 0.049804688 to 1
- hot_moment_scales: float32 [4096], P('row'), may hold values from 0.05 to 2
- hot_second_scales: float32 [4096], P('row'), may hold values from 0.01 to 1
Outputs:
- cold_table_new: float32 [32768, 256], P(('dp', 'row'))
- cold_moment_codes_new: bfloat16 [32768, 256], P(('dp', 'row'))
- cold_second_codes_new: bfloat16 [32768, 256], P(('dp', 'row'))
- cold_moment_scales_new: float32 [32768], P(('dp', 'row'))
- cold_second_scales_new: float32 [32768], P(('dp', 'row'))
- hot_replica: float32 [4096, 256], replicated
- hot_moment_codes_new: bfloat16 [4096, 256], P('row')
- hot_second_codes_new: bfloat16 [4096, 256], P('row')
- hot_moment_scales_new: float32 [4096], P('row')
- hot_second_scales_new: float32 [4096], P('row')
The draws below stay inside these ranges and needn't reach their ends.
Inputs may be any that keep to these rules, and one draw needn't show every extreme that they name: `bag_index`: each device's rows of samples name every value below 128 at least once; a value v of 128 or more names hot row v - 128. `owner_counts`: row k belongs to device k; its entries, one for each owning device in order along dp then row, sum to 128; some owner gets 8 from every device. `touched_ids`: row k lists device k's touched rows grouped by owner in owner order, owner o's group holding owner_counts[k, o] entries; entries within a group are distinct.
All inputs are finite; a program needn't handle non-finite values.
Results may differ from the reference program's by a relative error of at most 0.001.
Values may be sent and summed in bfloat16 or wider, within the bound.
No kernel may reach another device: no remote copies, remote signals or barrier semaphores. Data moves between devices by JAX's collectives and lax.ppermute only.
A program may use at most 128 MiB of HBM per device.

```python
import math
import jax
import jax.numpy as jnp
from jax import lax

E = 256
POOL = 16
CAP = 8
OWN = 1024
SAMP_DEV = 512
OWNERS = 32
TOUCH_DEV = 128
HOT = 4096
SLAB = 32768
SAMPLES = 16384
N_DP = 4
N_ROW = 8


def touch_layout(key):
    owners = OWNERS
    key_list = jax.random.split(jax.random.fold_in(key, 71), 4)
    full_owner = jax.random.randint(key_list[0], (), 0, owners)
    cell_count = (owners - 1) * (CAP - 1)
    spare_units = TOUCH_DEV - CAP - (owners - 1)
    ranking = jax.vmap(lambda subkey: jax.random.permutation(subkey, cell_count))(jax.random.split(key_list[1], owners))
    chosen = (ranking < spare_units).astype(jnp.int32).reshape(owners, owners - 1, CAP - 1)
    others = 1 + jnp.sum(chosen, axis=2)
    shifted = jnp.concatenate([jnp.full((owners, 1), CAP, jnp.int32), others.astype(jnp.int32)], axis=1)
    offset = (jnp.arange(owners, dtype=jnp.int32) - full_owner) % owners
    counts = shifted[:, offset].astype(jnp.int32)
    run_end = jnp.cumsum(counts, axis=1).astype(jnp.int32)
    starts = run_end - counts
    positions = jnp.arange(TOUCH_DEV, dtype=jnp.int32)
    owner_of = jax.vmap(lambda limits: jnp.searchsorted(limits, positions, side='right'))(run_end).astype(jnp.int32)
    within = positions[None, :] - jnp.take_along_axis(starts, owner_of, axis=1)
    base_offset = jax.random.randint(key_list[2], (owners, owners), 0, OWN)
    shuffle = jax.vmap(lambda subkey: jax.random.permutation(subkey, OWN))(jax.random.split(key_list[3], owners))
    slot_index = (jnp.take_along_axis(base_offset, owner_of, axis=1) + within) % OWN
    row_ids = jnp.take_along_axis(shuffle, slot_index.astype(jnp.int32), axis=1)
    return (counts, row_ids.astype(jnp.int32))


def draw_owner_counts(key, part):
    return touch_layout(key)[0]


def draw_touched_ids(key, part):
    return touch_layout(key)[1]


def draw_bag_index(key, part):
    owners = OWNERS
    entries = SAMP_DEV * POOL
    key_list = jax.random.split(jax.random.fold_in(key, 13), 6)
    hot_order = jax.random.permutation(key_list[0], HOT).astype(jnp.int32)
    ranking = jax.vmap(lambda subkey: jax.random.permutation(subkey, entries))(jax.random.split(key_list[1], owners)).astype(jnp.int32)
    cold_pick = jax.random.randint(key_list[2], (owners, entries), 0, TOUCH_DEV)
    coin_flip = jax.random.randint(key_list[3], (owners, entries), 0, 2)
    first_factor = jax.random.randint(key_list[4], (owners, entries), 0, HOT)
    second_factor = jax.random.randint(key_list[5], (owners, entries), 0, HOT)
    hot_pick = hot_order[first_factor * second_factor // HOT]
    values = jnp.where(ranking < TOUCH_DEV, ranking, jnp.where(coin_flip == 1, TOUCH_DEV + hot_pick, cold_pick))
    return values.reshape(owners * SAMP_DEV, POOL).astype(jnp.int32)


def block_scale(own_key, shape, pieces, least, top_value):
    gain, own = 1.0, jax.random.fold_in(own_key, 6)
    for position, blocks in pieces:
        heights = jnp.exp(jax.random.uniform(jax.random.fold_in(own, position), (blocks,), jnp.float32, least / len(pieces), top_value / len(pieces)))
        gain = gain * jnp.repeat(heights, shape[position] // blocks).reshape([-1 if axis == position else 1 for axis in range(len(shape))])
    return gain


def normal_values(stream_key, shape, width, reach, pieces=(), held_as=jnp.bfloat16):
    factor_of = block_scale(stream_key, shape, pieces, -0.22, 0.18) if pieces else 1.0
    array = jax.random.normal(stream_key, shape, jnp.float32) * width * factor_of
    return jnp.minimum(jnp.maximum(array, -reach), reach).astype(held_as)


def setup_inputs(seed: int = 0) -> dict:
    streams_of = jax.random.split(jax.random.key(seed), 15)
    return {
        "bag_index": draw_bag_index(jax.random.fold_in(streams_of[14], 71), 0),
        "pooled_grad": normal_values(streams_of[1], (SAMPLES, E), 1.0, 6.0, ((0, 32),)),
        "touched_ids": draw_touched_ids(jax.random.fold_in(streams_of[14], 71), 0),
        "owner_counts": draw_owner_counts(jax.random.fold_in(streams_of[14], 71), 0),
        "cold_table": normal_values(streams_of[4], (SLAB, E), 1.0, 6.0, ((0, 32),), jnp.float32),
        "cold_moment_codes": jnp.clip(jax.random.uniform(streams_of[5], (SLAB, E), jnp.float32, -1.0, 1.0) * block_scale(streams_of[5], (SLAB, E), ((0, 32),), -0.4, 0.0), -1.0, 1.0).astype(jnp.bfloat16),
        "cold_second_codes": jnp.clip(0.049804688 + 0.9501953 * jax.random.uniform(streams_of[6], (SLAB, E), jnp.float32) ** block_scale(streams_of[6], (SLAB, E), ((0, 32),), -0.2, 0.2), 0.049804688, 1.0).astype(jnp.bfloat16),
        "cold_moment_scales": jnp.clip(jnp.exp(math.log(2.0) - 3.6888794 * jax.random.uniform(streams_of[7], (SLAB,), jnp.float32) ** block_scale(streams_of[7], (SLAB,), ((0, 32),), -0.2, 0.2)), 0.05, 2.0),
        "cold_second_scales": jnp.clip(jnp.exp(math.log(1.0) - 4.6051702 * jax.random.uniform(streams_of[8], (SLAB,), jnp.float32) ** block_scale(streams_of[8], (SLAB,), ((0, 32),), -0.2, 0.2)), 0.01, 1.0),
        "hot_table": normal_values(streams_of[9], (HOT, E), 1.0, 6.0, (), jnp.float32),
        "hot_moment_codes": jnp.clip(jax.random.uniform(streams_of[10], (HOT, E), jnp.float32, -1.0, 1.0) * block_scale(streams_of[10], (HOT, E), ((0, 8),), -0.4, 0.0), -1.0, 1.0).astype(jnp.bfloat16),
        "hot_second_codes": jnp.clip(0.049804688 + 0.9501953 * jax.random.uniform(streams_of[11], (HOT, E), jnp.float32) ** block_scale(streams_of[11], (HOT, E), ((0, 8),), -0.2, 0.2), 0.049804688, 1.0).astype(jnp.bfloat16),
        "hot_moment_scales": jnp.clip(jnp.exp(math.log(2.0) - 3.6888794 * jax.random.uniform(streams_of[12], (HOT,), jnp.float32) ** block_scale(streams_of[12], (HOT,), ((0, 8),), -0.2, 0.2)), 0.05, 2.0),
        "hot_second_scales": jnp.clip(jnp.exp(math.log(1.0) - 4.6051702 * jax.random.uniform(streams_of[13], (HOT,), jnp.float32) ** block_scale(streams_of[13], (HOT,), ((0, 8),), -0.2, 0.2)), 0.01, 1.0),
    }


beta_one = 0.9
beta_two = 0.999
learn_rate = 0.1
adam_eps = 1e-08
bias_one = 1.0 - 1.7478712517226947e-46
bias_two = 0.6323045752290363

def adam_rows(weights, moment_codes, second_codes, moment_scales, second_scales, gradient):
    moment = beta_one * moment_scales[:, None] * moment_codes.astype(jnp.float32) + (1.0 - beta_one) * gradient
    second = beta_two * second_scales[:, None] * second_codes.astype(jnp.float32) + (1.0 - beta_two) * gradient * gradient
    updated = weights - learn_rate * (moment / bias_one) / (jnp.sqrt(second / bias_two) + adam_eps)
    moment_scale_new = lax.optimization_barrier(jnp.max(jnp.abs(moment), axis=1)) + 1e-06
    second_scale_new = lax.optimization_barrier(jnp.max(second, axis=1)) + 1e-06
    moment_code_new = (moment / moment_scale_new[:, None]).astype(jnp.bfloat16)
    second_code_new = (second / second_scale_new[:, None]).astype(jnp.bfloat16)
    return (updated, moment_code_new, second_code_new, moment_scale_new, second_scale_new)

def reference(bag_index, pooled_grad, touched_ids, owner_counts, cold_table, cold_moment_codes, cold_second_codes, cold_moment_scales, cold_second_scales, hot_table, hot_moment_codes, hot_second_codes, hot_moment_scales, hot_second_scales):
    owners = N_DP * N_ROW
    local_rows = TOUCH_DEV + HOT
    bags_split = bag_index.reshape(owners, SAMP_DEV, POOL)
    grads_split = pooled_grad.reshape(owners, SAMP_DEV, E)
    positions = jnp.arange(TOUCH_DEV, dtype=jnp.int32)
    columns = jnp.arange(local_rows, dtype=jnp.int32)

    def visit(carry, inputs):
        cold_sum, hot_sum = carry
        bag_rows, grad_rows, id_row, count_row = inputs
        tally = jnp.zeros((SAMP_DEV, local_rows), jnp.float32)
        for entry in range(POOL):
            tally = tally + (bag_rows[:, entry][:, None] == columns[None, :]).astype(jnp.float32)
        local_grad = jnp.dot(tally.T.astype(jnp.bfloat16), grad_rows, preferred_element_type=jnp.float32)
        run_end = jnp.cumsum(count_row).astype(jnp.int32)
        owner = lax.optimization_barrier(jnp.sum((run_end[None, :] <= positions[:, None]).astype(jnp.int32), axis=1)).astype(jnp.int32)
        target = (owner * OWN + id_row).astype(jnp.int32)
        cold_sum = cold_sum.at[target].add(local_grad[:TOUCH_DEV])
        hot_sum = hot_sum + local_grad[TOUCH_DEV:]
        return ((cold_sum, hot_sum), None)
    start = (jnp.zeros((owners * OWN, E), jnp.float32), jnp.zeros((HOT, E), jnp.float32))
    (cold_grad, hot_grad), _ = lax.scan(visit, start, (bags_split, grads_split, touched_ids, owner_counts))
    cold = adam_rows(cold_table, cold_moment_codes, cold_second_codes, cold_moment_scales, cold_second_scales, cold_grad)
    hot = adam_rows(hot_table, hot_moment_codes, hot_second_codes, hot_moment_scales, hot_second_scales, hot_grad)
    return (cold[0], cold[1], cold[2], cold[3], cold[4], hot[0], hot[1], hot[2], hot[3], hot[4])
```

```python
import functools

import jax
import jax.numpy as jnp
from jax import lax
from jax.experimental import pallas as pl
from jax.experimental.pallas import tpu as pltpu
from jax.sharding import PartitionSpec as P

CAP = 8
CORES = 2
META = 16
GROUPS = 8
STEP = 0.125
TOP = 32767.0

beta_one = 0.9
beta_two = 0.999
learn_rate = 0.1
adam_eps = 1e-08
bias_one = 1.0 - 1.7478712517226947e-46
bias_two = 0.6323045752290363

f32, bf16, i32, i16 = jnp.float32, jnp.bfloat16, jnp.int32, jnp.int16


def log2_of(n):
    assert n & (n - 1) == 0, n
    return n.bit_length() - 1


def iota(shape, dim):
    return lax.broadcasted_iota(i32, shape, dim)


def row_codes(x):
    top = jnp.maximum(jnp.max(jnp.abs(x), axis=1, keepdims=True), 1e-30)
    power = jnp.ceil(jnp.log(top) * (1.4426950408889634 / STEP))
    scaled = x * (jnp.exp2(power * -STEP) * TOP)
    rounded = jnp.floor(scaled + 0.5)
    return jnp.clip(rounded, -TOP, TOP).astype(i32), power


def row_values(codes, power):
    return codes.astype(i32).astype(f32) * (jnp.exp2(power * STEP) * (1.0 / TOP))


def to_row(column, lanes, first=0):
    n = column.shape[0]
    hit = iota((n, lanes), 0) + first == iota((n, lanes), 1)
    return jnp.sum(jnp.where(hit, column, 0.0), axis=0, keepdims=True)


def to_column(row, n):
    lanes = row.shape[1]
    hit = iota((n, lanes), 0) == iota((n, lanes), 1)
    return jnp.sum(jnp.where(hit, row, 0.0), axis=1, keepdims=True)


def stack_rows(rows, height, lanes):
    place = iota((height, lanes), 0)
    out = jnp.zeros((height, lanes), f32)
    for index, row in enumerate(rows):
        out = out + jnp.where(place == index, row, 0.0)
    return out


def gradient_kernel(dims, where_ref, *refs):
    sources, z_size, dp_size, touch, owners, sub, pool = dims
    row_size = z_size * CORES
    pooled_refs = refs[:sources]
    ints_refs = refs[sources : 2 * sources]
    hot_refs = refs[2 * sources : 2 * sources + z_size]
    cold_refs = refs[2 * sources + z_size : 2 * sources + 2 * z_size]
    tally_ref, hot_ref, cold_ref = refs[2 * sources + 2 * z_size :]
    samples, features = pooled_refs[0].shape
    my_dp, my_z, my_core = where_ref[0], where_ref[1], where_ref[2]
    local = z_size * sub
    group = local // GROUPS
    cell = CAP * z_size
    slots = sources * CAP
    width = min(samples, 256)
    place = iota((group, width), 0)
    ids_sum = jnp.zeros((cell, features), f32)
    powers_sum = jnp.zeros((cell, features), f32)
    cell_z = jnp.bitwise_xor(iota((cell, 1), 0) >> log2_of(CAP), my_z)
    cell_owner = my_dp * row_size + cell_z * CORES + my_core
    cell_slot = iota((cell, 1), 0) & (CAP - 1)
    for source in range(sources):
        ints = ints_refs[source][...].astype(i32)
        grads = pooled_refs[source][...]
        bag = ints[:pool, :samples]
        hot = bag - touch
        in_block = hot & (sub * dp_size - 1)
        owner_row = hot >> log2_of(sub * dp_size)
        mine = (
            (hot >= 0)
            & ((in_block >> log2_of(sub)) == my_dp)
            & ((owner_row & (CORES - 1)) == my_core)
        )
        target = jnp.bitwise_xor(owner_row >> log2_of(CORES), my_z) * sub + (in_block & (sub - 1))
        high = target & (group - 1)
        digit = jnp.where(
            mine, jnp.left_shift(jnp.ones_like(target), (target >> log2_of(group)) * 4), 0
        )
        for first in range(0, samples, width):
            even = jnp.zeros((group, width), i32)
            odd = jnp.zeros((group, width), i32)
            for entry in range(0, pool, 8):
                packed = jnp.zeros((group, width), i32)
                for j in range(entry, min(entry + 8, pool)):
                    packed = packed + jnp.where(
                        place == high[j : j + 1, first : first + width],
                        digit[j : j + 1, first : first + width],
                        0,
                    )
                even = even + (packed & 0x0F0F0F0F)
                odd = odd + ((packed >> 4) & 0x0F0F0F0F)
            for k in range(GROUPS):
                count = ((odd if k % 2 else even) >> (8 * (k // 2))) & 0xFF
                tally_ref[k * group : (k + 1) * group, first : first + width] = count.astype(
                    f32
                ).astype(bf16)
        product = jnp.dot(tally_ref[...], grads, preferred_element_type=f32)
        if source == 0:
            hot_ref[...] = product
        else:
            hot_ref[...] += product

        counts = ints[pool + 1 : pool + 2, :owners].astype(f32)
        lane = iota((cell, owners), 1)
        run_start = jnp.sum(jnp.where(lane < cell_owner, counts, 0.0), axis=1, keepdims=True)
        run_count = jnp.sum(jnp.where(lane == cell_owner, counts, 0.0), axis=1, keepdims=True)
        live = cell_slot.astype(f32) < run_count
        position = jnp.where(live, run_start + cell_slot.astype(f32), -1.0).astype(i32)
        names = ints[pool : pool + 1, :touch].astype(f32)
        ids = jnp.sum(
            jnp.where(iota((cell, touch), 1) == position, names, 0.0), axis=1, keepdims=True
        )
        tally = jnp.zeros((cell, samples), f32)
        for j in range(pool):
            tally = tally + jnp.where(position == bag[j : j + 1, :], 1.0, 0.0)
        rows = jnp.dot(tally.astype(bf16), grads, preferred_element_type=f32)
        codes, powers = row_codes(rows)
        for k in range(z_size):
            cold_ref[k, source * CAP : (source + 1) * CAP, :] = codes[k * CAP : (k + 1) * CAP]
        hit = iota((cell, features), 1) == cell_slot + source * CAP
        ids_sum = ids_sum + jnp.where(hit, ids, 0.0)
        powers_sum = powers_sum + jnp.where(hit, powers, 0.0)

    for k in range(z_size):
        codes, powers = row_codes(hot_ref[k * sub : (k + 1) * sub, :])
        hot_refs[k][:sub, :] = codes.astype(i16)
        hot_refs[k][sub:, :] = (
            stack_rows([to_row(powers, features)], META, features).astype(i32).astype(i16)
        )
        cold_refs[k][:slots, :] = cold_ref[k].astype(i16)
        rows = [
            jnp.sum(ids_sum[k * CAP : (k + 1) * CAP], axis=0, keepdims=True),
            jnp.sum(powers_sum[k * CAP : (k + 1) * CAP], axis=0, keepdims=True),
        ]
        cold_refs[k][slots:, :] = stack_rows(rows, META, features).astype(i32).astype(i16)


def moments(gradient, moment_codes, second_codes, moment_scale, second_scale):
    moment = beta_one * moment_scale * moment_codes.astype(f32) + (1.0 - beta_one) * gradient
    second = (
        beta_two * second_scale * second_codes.astype(f32)
        + (1.0 - beta_two) * gradient * gradient
    )
    update = learn_rate * (moment / bias_one) / (jnp.sqrt(second / bias_two) + adam_eps)
    moment_scale_new = jnp.max(jnp.abs(moment), axis=1, keepdims=True) + 1e-06
    second_scale_new = jnp.max(second, axis=1, keepdims=True) + 1e-06
    return (
        update,
        (moment / moment_scale_new).astype(bf16),
        (second / second_scale_new).astype(bf16),
        moment_scale_new,
        second_scale_new,
    )


def three_parts(x):
    first = x.astype(bf16).astype(f32)
    second = (x - first).astype(bf16).astype(f32)
    return [first, second, x - first - second]


def hot_kernel(z_size, where_ref, *refs):
    parts = refs[:z_size]
    mc_ref, vc_ref, ms_ref, vs_ref, update_ref, codes_ref = refs[z_size:]
    sub, features = mc_ref.shape
    my_dp = where_ref[0]
    gradient = jnp.zeros((sub, features), f32)
    for part in parts:
        power = part[sub:, :].astype(i32).astype(f32)[:1]
        gradient = gradient + row_values(part[:sub, :], to_column(power, sub))
    update, mc, vc, ms, vs = moments(
        gradient,
        mc_ref[...],
        vc_ref[...],
        to_column(ms_ref[pl.ds(my_dp, 1), :], sub),
        to_column(vs_ref[pl.ds(my_dp, 1), :], sub),
    )
    codes, powers = row_codes(update)
    update_ref[:sub, :] = codes.astype(i16)
    update_ref[sub:, :] = (
        stack_rows([to_row(powers, features)], META, features).astype(i32).astype(i16)
    )
    codes_ref[:sub, :] = mc
    codes_ref[sub : 2 * sub, :] = vc
    rows = three_parts(to_row(ms, features)) + three_parts(to_row(vs, features))
    codes_ref[2 * sub :, :] = stack_rows(rows, META, features).astype(bf16)


def spread_kernel(dp_size, where_ref, *refs):
    parts = refs[:dp_size]
    mc_ref, vc_ref, ms_ref, vs_ref = refs[dp_size:]
    sub = mc_ref.shape[0] // dp_size
    for k in range(dp_size):
        owner = jnp.bitwise_xor(where_ref[0], k)
        start = pl.multiple_of(owner * sub, sub)
        mc_ref[pl.ds(start, sub), :] = parts[k][:sub, :]
        vc_ref[pl.ds(start, sub), :] = parts[k][sub : 2 * sub, :]
        rows = parts[k][2 * sub :, :].astype(f32)
        ms_ref[pl.ds(owner, 1), :] = (rows[0:1] + rows[1:2] + rows[2:3])[:, :sub]
        vs_ref[pl.ds(owner, 1), :] = (rows[3:4] + rows[4:5] + rows[5:6])[:, :sub]


def cold_kernel(z_size, where_ref, *refs):
    parts = refs[:z_size]
    table_ref, mc_ref, vc_ref, ms_ref, vs_ref = refs[z_size : z_size + 5]
    new_ref, mcn_ref, vcn_ref, msn_ref, vsn_ref = refs[z_size + 5 : z_size + 10]
    coarse_ref, fine_ref, ids_ref = refs[z_size + 10 :]
    block, features = table_ref.shape
    slots = parts[0].shape[0] - META

    @pl.when(pl.program_id(0) == 0)
    def _():
        for k, part in enumerate(parts):
            meta = part[slots:, :].astype(i32).astype(f32)
            value = row_values(part[:slots, :], to_column(meta[1:2], slots))
            coarse = value.astype(bf16)
            coarse_ref[k * slots : (k + 1) * slots, :] = coarse
            fine_ref[k * slots : (k + 1) * slots, :] = (value - coarse.astype(f32)).astype(bf16)
            ids_ref[k : k + 1, :] = meta[0:1].astype(i32)

    first = pl.program_id(0) * block
    gradient = jnp.zeros((block, features), f32)
    for k in range(z_size):
        pick = iota((block, slots), 0) + first == ids_ref[k : k + 1, :slots]
        pick = jnp.where(pick, 1.0, 0.0).astype(bf16)
        gradient = gradient + jnp.dot(
            pick, coarse_ref[k * slots : (k + 1) * slots, :], preferred_element_type=f32
        )
        gradient = gradient + jnp.dot(
            pick, fine_ref[k * slots : (k + 1) * slots, :], preferred_element_type=f32
        )
    row = pl.ds(pl.program_id(0), 1)
    update, mc, vc, ms, vs = moments(
        gradient,
        mc_ref[...],
        vc_ref[...],
        to_column(ms_ref[row, :], block),
        to_column(vs_ref[row, :], block),
    )
    new_ref[...] = table_ref[...] - update
    mcn_ref[...] = mc
    vcn_ref[...] = vc
    msn_ref[row, :] = to_row(ms, block)
    vsn_ref[row, :] = to_row(vs, block)


def replica_kernel(dp_size, where_ref, *refs):
    parts = refs[: CORES * dp_size]
    table_ref, new_ref = refs[CORES * dp_size :]
    sub = parts[0].shape[1] - META
    for core in range(CORES):
        for k in range(dp_size):
            owner = jnp.bitwise_xor(where_ref[2], core) * dp_size + jnp.bitwise_xor(where_ref[0], k)
            rows = pl.ds(pl.multiple_of(owner * sub, sub), sub)
            part = parts[core * dp_size + k]
            power = part[0, sub:, :].astype(i32).astype(f32)[:1]
            new_ref[rows, :] = table_ref[rows, :] - row_values(
                part[0, :sub, :], to_column(power, sub)
            )


VMEM = pltpu.VMEM


def whole(memory_space=VMEM):
    return pl.BlockSpec(memory_space=memory_space)


def send(x, axis, flip):
    size = lax.axis_size(axis)
    return lax.ppermute(x, axis, [(i, i ^ flip) for i in range(size)])


def body(
    bag_index,
    pooled_grad,
    touched_ids,
    owner_counts,
    cold_table,
    cold_moment_codes,
    cold_second_codes,
    cold_moment_scales,
    cold_second_scales,
    hot_table,
    hot_moment_codes,
    hot_second_codes,
    hot_moment_scales,
    hot_second_scales,
):
    dp_size = lax.axis_size("dp")
    row_size = lax.axis_size("row")
    z_size = row_size // CORES
    samples, pool = bag_index.shape
    features = pooled_grad.shape[1]
    touch = touched_ids.shape[1]
    owners = owner_counts.shape[1]
    hot_rows = hot_table.shape[0]
    owned = cold_table.shape[0]
    sub = hot_rows // row_size // dp_size
    sources = CORES * dp_size
    slots = sources * CAP
    row = lax.axis_index("row")
    here = jnp.stack([lax.axis_index("dp"), row // CORES, row % CORES]).astype(i32)

    width = max(samples, touch, owners)
    ints = jnp.concatenate(
        [
            jnp.pad(x, ((0, 0), (0, width - x.shape[1])))
            for x in (bag_index.T, touched_ids, owner_counts)
        ]
    ).astype(i16)
    pooled_list = [pooled_grad] + [send(pooled_grad, "dp", k) for k in range(1, dp_size)]
    ints_list = [ints] + [send(ints, "dp", k) for k in range(1, dp_size)]
    pooled_list = pooled_list + [send(x, "row", 1) for x in pooled_list]
    ints_list = ints_list + [send(x, "row", 1) for x in ints_list]

    dims = (sources, z_size, dp_size, touch, owners, sub, pool)
    outs = pl.pallas_call(
        functools.partial(gradient_kernel, dims),
        out_shape=[jax.ShapeDtypeStruct((sub + META, features), i16)] * z_size
        + [jax.ShapeDtypeStruct((slots + META, features), i16)] * z_size,
        in_specs=[whole(pltpu.SMEM)] + [whole()] * (2 * sources),
        out_specs=[whole()] * (2 * z_size),
        scratch_shapes=[
            VMEM((z_size * sub, samples), bf16),
            VMEM((z_size * sub, features), f32),
            VMEM((z_size, slots, features), i32),
        ],
        name="gradients",
    )(here, *pooled_list, *ints_list)
    hot_parts = [outs[0]] + [send(outs[k], "row", CORES * k) for k in range(1, z_size)]
    cold_out = outs[z_size:]
    cold_parts = [cold_out[0]] + [send(cold_out[k], "row", CORES * k) for k in range(1, z_size)]

    scalars = pltpu.PrefetchScalarGridSpec(
        num_scalar_prefetch=1,
        grid=(1,),
        in_specs=[pl.BlockSpec((sub + META, features), lambda i, w: (0, 0))] * z_size
        + [pl.BlockSpec((sub, features), lambda i, w: (w[0], 0))] * 2
        + [pl.BlockSpec((dp_size, sub), lambda i, w: (0, 0))] * 2,
        out_specs=[
            pl.BlockSpec((sub + META, features), lambda i, w: (0, 0)),
            pl.BlockSpec((2 * sub + META, features), lambda i, w: (0, 0)),
        ],
    )
    update, codes = pl.pallas_call(
        functools.partial(hot_kernel, z_size),
        out_shape=[
            jax.ShapeDtypeStruct((sub + META, features), i16),
            jax.ShapeDtypeStruct((2 * sub + META, features), bf16),
        ],
        grid_spec=scalars,
        name="hot_rows",
    )(
        here,
        *hot_parts,
        hot_moment_codes,
        hot_second_codes,
        hot_moment_scales.reshape(dp_size, sub),
        hot_second_scales.reshape(dp_size, sub),
    )
    column = jnp.stack([update] + [send(update, "row", CORES * k) for k in range(1, z_size)])
    code_parts = [codes] + [send(codes, "dp", k) for k in range(1, dp_size)]
    plane = [column] + [send(column, "dp", k) for k in range(1, dp_size)]
    plane = plane + [send(x, "row", 1) for x in plane]

    hot_mc, hot_vc, hot_ms, hot_vs = pl.pallas_call(
        functools.partial(spread_kernel, dp_size),
        out_shape=[jax.ShapeDtypeStruct((dp_size * sub, features), bf16)] * 2
        + [jax.ShapeDtypeStruct((dp_size, sub), f32)] * 2,
        in_specs=[whole(pltpu.SMEM)] + [whole()] * dp_size,
        out_specs=[whole()] * 4,
        name="spread_codes",
    )(here, *code_parts)

    block = min(128, owned)
    blocks = owned // block
    by_rows = pl.BlockSpec((block, features), lambda i, w: (i, 0))
    by_scales = pl.BlockSpec((blocks, block), lambda i, w: (0, 0))
    cold = pl.pallas_call(
        functools.partial(cold_kernel, z_size),
        out_shape=[
            jax.ShapeDtypeStruct((owned, features), f32),
            jax.ShapeDtypeStruct((owned, features), bf16),
            jax.ShapeDtypeStruct((owned, features), bf16),
            jax.ShapeDtypeStruct((blocks, block), f32),
            jax.ShapeDtypeStruct((blocks, block), f32),
        ],
        grid_spec=pltpu.PrefetchScalarGridSpec(
            num_scalar_prefetch=1,
            grid=(blocks,),
            in_specs=[pl.BlockSpec((slots + META, features), lambda i, w: (0, 0))] * z_size
            + [by_rows] * 3
            + [by_scales] * 2,
            out_specs=[by_rows] * 3 + [by_scales] * 2,
            scratch_shapes=[
                VMEM((z_size * slots, features), bf16),
                VMEM((z_size * slots, features), bf16),
                VMEM((max(z_size, 8), features), i32),
            ],
        ),
        name="cold_rows",
    )(
        here,
        *cold_parts,
        cold_table,
        cold_moment_codes,
        cold_second_codes,
        cold_moment_scales.reshape(blocks, block),
        cold_second_scales.reshape(blocks, block),
    )

    tall = CORES * dp_size * sub
    layer = pl.BlockSpec((tall, features), lambda i, w: (jnp.bitwise_xor(i, w[1]), 0))
    replica = pl.pallas_call(
        functools.partial(replica_kernel, dp_size),
        out_shape=jax.ShapeDtypeStruct((hot_rows, features), f32),
        grid_spec=pltpu.PrefetchScalarGridSpec(
            num_scalar_prefetch=1,
            grid=(z_size,),
            in_specs=[pl.BlockSpec((1, sub + META, features), lambda i, w: (i, 0, 0))]
            * (CORES * dp_size)
            + [layer],
            out_specs=layer,
        ),
        name="replica",
    )(here, *plane, hot_table)
    return (
        cold[0],
        cold[1],
        cold[2],
        cold[3].reshape(owned),
        cold[4].reshape(owned),
        replica,
        hot_mc,
        hot_vc,
        hot_ms.reshape(dp_size * sub),
        hot_vs.reshape(dp_size * sub),
    )


def solution(mesh):
    return jax.shard_map(
        body,
        mesh=mesh,
        in_specs=(
            P(("dp", "row"), None),
            P(("dp", "row"), None),
            P(("dp", "row"), None),
            P(("dp", "row"), None),
            P(("dp", "row"), None),
            P(("dp", "row"), None),
            P(("dp", "row"), None),
            P(("dp", "row")),
            P(("dp", "row")),
            P(),
            P("row", None),
            P("row", None),
            P("row"),
            P("row"),
        ),
        out_specs=(
            P(("dp", "row"), None),
            P(("dp", "row"), None),
            P(("dp", "row"), None),
            P(("dp", "row")),
            P(("dp", "row")),
            P(),
            P("row", None),
            P("row", None),
            P("row"),
            P("row"),
        ),
        check_vma=False,
    )
```

```python
import functools

import jax
import jax.numpy as jnp
from jax import lax
from jax.experimental import pallas as pl
from jax.experimental.pallas import tpu as pltpu
from jax.sharding import PartitionSpec as P


CAP = 8
CORES = 2
META = 16
GROUPS = 8
STEP = 0.125
TOP = 32767.0

beta_one = 0.9
beta_two = 0.999
learn_rate = 0.1
adam_eps = 1e-08
bias_one = 1.0 - 1.7478712517226947e-46
bias_two = 0.6323045752290363

f32, bf16, i32, i16 = jnp.float32, jnp.bfloat16, jnp.int32, jnp.int16


def log2_of(n):
    assert n & (n - 1) == 0, n
    return n.bit_length() - 1


def iota(shape, dim):
    return lax.broadcasted_iota(i32, shape, dim)


def row_codes(x):
    top = jnp.maximum(jnp.max(jnp.abs(x), axis=1, keepdims=True), 1e-30)
    power = jnp.ceil(jnp.log(top) * (1.4426950408889634 / STEP))
    scaled = x * (jnp.exp2(power * -STEP) * TOP)
    rounded = jnp.floor(scaled + 0.5)
    return jnp.clip(rounded, -TOP, TOP).astype(i32), power


def row_values(codes, power):
    return codes.astype(i32).astype(f32) * (jnp.exp2(power * STEP) * (1.0 / TOP))


def to_row(column, lanes, first=0):
    n = column.shape[0]
    hit = iota((n, lanes), 0) + first == iota((n, lanes), 1)
    return jnp.sum(jnp.where(hit, column, 0.0), axis=0, keepdims=True)


def to_column(row, n):
    lanes = row.shape[1]
    hit = iota((n, lanes), 0) == iota((n, lanes), 1)
    return jnp.sum(jnp.where(hit, row, 0.0), axis=1, keepdims=True)


def stack_rows(rows, height, lanes):
    place = iota((height, lanes), 0)
    out = jnp.zeros((height, lanes), f32)
    for index, row in enumerate(rows):
        out = out + jnp.where(place == index, row, 0.0)
    return out


def place_of(axis_names=("dp", "row")):
    row = lax.axis_index(axis_names[1])
    return lax.axis_index(axis_names[0]), row >> log2_of(CORES), row & (CORES - 1)


def pack_kernel(bag_hbm, ids_hbm, counts_hbm, out_ref, bag_ref, ids_ref, counts_ref, sems):
    copies = [
        pltpu.make_async_copy(source, target, sems.at[i])
        for i, (source, target) in enumerate(
            ((bag_hbm, bag_ref), (ids_hbm, ids_ref), (counts_hbm, counts_ref))
        )
    ]
    for copy in copies:
        copy.start()
    pool, samples = bag_ref.shape
    height, lanes = out_ref.shape
    out_ref[...] = jnp.zeros((height, lanes), i16)
    for copy in copies:
        copy.wait()
    out_ref[:pool, :samples] = bag_ref[...].astype(i16)
    rows = []
    for ref in (ids_ref, counts_ref):
        row = ref[...]
        if row.shape[1] < lanes:
            fill = jnp.zeros((1, lanes - row.shape[1]), i32)
            row = jnp.concatenate([row, fill], axis=1)
        rows.append(row)
    place = iota((height - pool, lanes), 0)
    tail = jnp.where(place == 0, rows[0], jnp.where(place == 1, rows[1], 0))
    out_ref[pool:, :] = tail.astype(i16)


def tally_kernel(dims, *refs):
    sources, z_size, dp_size, touch, owners, sub, pool, samples, features = dims
    row_size = z_size * CORES
    ints_refs = refs[:sources]
    pooled_hbm, tally_ref, ids_ref, pooled_ref, sem = refs[sources:]
    fetch = pltpu.make_async_copy(pooled_hbm, pooled_ref, sem)
    fetch.start()
    my_dp, my_z, my_core = place_of()
    local = z_size * sub
    group = local // GROUPS
    cell = CAP * z_size
    width = min(samples, 256)
    place = iota((group, width), 0)
    ids_sum = jnp.zeros((cell, features), f32)
    cell_z = jnp.bitwise_xor(iota((cell, 1), 0) >> log2_of(CAP), my_z)
    cell_owner = my_dp * row_size + cell_z * CORES + my_core
    cell_slot = iota((cell, 1), 0) & (CAP - 1)
    for source in range(sources):
        ints = ints_refs[source][...].astype(i32)
        bag = ints[:pool, :samples]
        hot = bag - touch
        in_block = hot & (sub * dp_size - 1)
        owner_row = hot >> log2_of(sub * dp_size)
        mine = (
            (hot >= 0)
            & ((in_block >> log2_of(sub)) == my_dp)
            & ((owner_row & (CORES - 1)) == my_core)
        )
        target = jnp.bitwise_xor(owner_row >> log2_of(CORES), my_z) * sub + (in_block & (sub - 1))
        high = target & (group - 1)
        digit = jnp.where(
            mine, jnp.left_shift(jnp.ones_like(target), (target >> log2_of(group)) * 4), 0
        )
        counts = ints[pool + 1 : pool + 2, :owners].astype(f32)
        lane = iota((cell, owners), 1)
        run_start = jnp.sum(jnp.where(lane < cell_owner, counts, 0.0), axis=1, keepdims=True)
        run_count = jnp.sum(jnp.where(lane == cell_owner, counts, 0.0), axis=1, keepdims=True)
        live = cell_slot.astype(f32) < run_count
        position = jnp.where(live, run_start + cell_slot.astype(f32), -1.0).astype(i32)
        names = ints[pool : pool + 1, :touch].astype(f32)
        ids = jnp.sum(
            jnp.where(iota((cell, touch), 1) == position, names, 0.0), axis=1, keepdims=True
        )
        hit = iota((cell, features), 1) == cell_slot + source * CAP
        ids_sum = ids_sum + jnp.where(hit, ids, 0.0)
        for first in range(0, samples, width):
            even = jnp.zeros((group, width), i32)
            odd = jnp.zeros((group, width), i32)
            cold = jnp.zeros((cell, width), i32)
            for entry in range(0, pool, 8):
                packed = jnp.zeros((group, width), i32)
                for j in range(entry, min(entry + 8, pool)):
                    packed = packed + jnp.where(
                        place == high[j : j + 1, first : first + width],
                        digit[j : j + 1, first : first + width],
                        0,
                    )
                    cold = cold + jnp.where(
                        position == bag[j : j + 1, first : first + width], 1, 0
                    )
                even = even + (packed & 0x0F0F0F0F)
                odd = odd + ((packed >> 4) & 0x0F0F0F0F)
            for k in range(GROUPS):
                count = ((odd if k % 2 else even) >> (8 * (k // 2))) & 0xFF
                tally_ref[source, k * group : (k + 1) * group, first : first + width] = (
                    count.astype(f32).astype(bf16)
                )
            tally_ref[source, local:, first : first + width] = cold.astype(f32).astype(bf16)
    for k in range(z_size):
        ids_ref[k : k + 1, :] = jnp.sum(ids_sum[k * CAP : (k + 1) * CAP], axis=0, keepdims=True)
    fetch.wait()


def gradient_kernel(dims, *refs):
    sources, z_size, sub = dims
    pooled_refs = refs[:sources]
    tally_ref, ids_ref = refs[sources : sources + 2]
    refs = refs[sources + 2 :]
    hot_refs, cold_refs = refs[:z_size], refs[z_size : 2 * z_size]
    hot_ref, cold_ref = refs[2 * z_size :]
    features = pooled_refs[0].shape[1]
    local = z_size * sub
    cell = CAP * z_size
    slots = sources * CAP
    powers_sum = jnp.zeros((cell, features), f32)
    cell_slot = iota((cell, 1), 0) & (CAP - 1)
    for source in range(sources):
        product = jnp.dot(
            tally_ref[source], pooled_refs[source][...], preferred_element_type=f32
        )
        if source == 0:
            hot_ref[...] = product[:local]
        else:
            hot_ref[...] += product[:local]
        codes, powers = row_codes(product[local:])
        for k in range(z_size):
            cold_ref[k, source * CAP : (source + 1) * CAP, :] = codes[k * CAP : (k + 1) * CAP]
        hit = iota((cell, features), 1) == cell_slot + source * CAP
        powers_sum = powers_sum + jnp.where(hit, powers, 0.0)

    for k in range(z_size):
        codes, powers = row_codes(hot_ref[k * sub : (k + 1) * sub, :])
        hot_refs[k][:sub, :] = codes.astype(i16)
        hot_refs[k][sub:, :] = (
            stack_rows([to_row(powers, features)], META, features).astype(i32).astype(i16)
        )
        cold_refs[k][:slots, :] = cold_ref[k].astype(i16)
        rows = [
            ids_ref[k : k + 1, :],
            jnp.sum(powers_sum[k * CAP : (k + 1) * CAP], axis=0, keepdims=True),
        ]
        cold_refs[k][slots:, :] = stack_rows(rows, META, features).astype(i32).astype(i16)


def moments(gradient, moment_codes, second_codes, moment_scale, second_scale):
    moment = beta_one * moment_scale * moment_codes.astype(f32) + (1.0 - beta_one) * gradient
    second = (
        beta_two * second_scale * second_codes.astype(f32)
        + (1.0 - beta_two) * gradient * gradient
    )
    return moment, second


def update_of(moment, second):
    return learn_rate * (moment / bias_one) / (jnp.sqrt(second / bias_two) + adam_eps)


def new_codes(moment, second):
    moment_scale = jnp.max(jnp.abs(moment), axis=1, keepdims=True) + 1e-06
    second_scale = jnp.max(second, axis=1, keepdims=True) + 1e-06
    return (
        (moment * (1.0 / moment_scale)).astype(bf16),
        (second * (1.0 / second_scale)).astype(bf16),
        moment_scale,
        second_scale,
    )


def write_coded(ref, first, codes, powers):
    count, features = codes.shape
    ref[first : first + count, :] = codes.astype(i16)
    ref[first + count : first + count + META, :] = (
        stack_rows([to_row(powers, features)], META, features).astype(i32).astype(i16)
    )


def read_coded(ref, first, count):
    meta = ref[first + count : first + count + META, :].astype(i32).astype(f32)
    return row_values(ref[first : first + count, :], to_column(meta[:1], count))


def hot_kernel(z_size, *refs):
    parts = refs[:z_size]
    mc_ref, vc_ref, ms_ref, vs_ref, update_ref, both_ref = refs[z_size:]
    sub = parts[0].shape[0] - META
    my_dp, _, _ = place_of()
    gradient = read_coded(parts[0], 0, sub)
    for part in parts[1:]:
        gradient = gradient + read_coded(part, 0, sub)
    codes, powers = row_codes(gradient)
    write_coded(both_ref, sub + META, codes, powers)
    rows = pl.ds(pl.multiple_of(my_dp * sub, sub), sub)
    moment, second = moments(
        row_values(codes, powers),
        mc_ref[rows, :],
        vc_ref[rows, :],
        to_column(ms_ref[pl.ds(my_dp, 1), :], sub),
        to_column(vs_ref[pl.ds(my_dp, 1), :], sub),
    )
    codes, powers = row_codes(update_of(moment, second))
    write_coded(update_ref, 0, codes, powers)
    write_coded(both_ref, 0, codes, powers)


def join_kernel(*refs):
    parts, out_ref = refs[:-1], refs[-1]
    height = parts[0].shape[0]
    for k, part in enumerate(parts):
        out_ref[k * height : (k + 1) * height, :] = part[...]


def spread_kernel(dp_size, *refs):
    parts = refs[:dp_size]
    mc_ref, vc_ref, ms_ref, vs_ref, mcn_ref, vcn_ref, msn_ref, vsn_ref = refs[dp_size:]
    sub = mc_ref.shape[0] // dp_size
    my_dp, _, _ = place_of()
    for k, part in enumerate(parts):
        owner = jnp.bitwise_xor(my_dp, k)
        rows = pl.ds(pl.multiple_of(owner * sub, sub), sub)
        row = pl.ds(owner, 1)
        moment, second = moments(
            read_coded(part, sub + META, sub),
            mc_ref[rows, :],
            vc_ref[rows, :],
            to_column(ms_ref[row, :], sub),
            to_column(vs_ref[row, :], sub),
        )
        mc, vc, ms, vs = new_codes(moment, second)
        mcn_ref[rows, :] = mc
        vcn_ref[rows, :] = vc
        msn_ref[row, :] = to_row(ms, sub)
        vsn_ref[row, :] = to_row(vs, sub)


def fetch_kernel(source, target, sem):
    copy = pltpu.make_async_copy(source, target, sem)
    copy.start()
    copy.wait()


def cold_kernel(z_size, *refs):
    parts = refs[:z_size]
    table_ref, mc_ref, vc_ref, ms_ref, vs_ref = refs[z_size : z_size + 5]
    new_ref, mcn_ref, vcn_ref, msn_ref, vsn_ref = refs[z_size + 5 : z_size + 10]
    coarse_ref, fine_ref, ids_ref = refs[z_size + 10 :]
    block, features = table_ref.shape
    slots = parts[0].shape[0] - META

    @pl.when(pl.program_id(0) == 0)
    def _():
        for k, part in enumerate(parts):
            meta = part[slots:, :].astype(i32).astype(f32)
            value = row_values(part[:slots, :], to_column(meta[1:2], slots))
            coarse = value.astype(bf16)
            coarse_ref[k * slots : (k + 1) * slots, :] = coarse
            fine_ref[k * slots : (k + 1) * slots, :] = (value - coarse.astype(f32)).astype(bf16)
            ids_ref[k : k + 1, :] = meta[0:1].astype(i32)

    first = pl.program_id(0) * block
    gradient = jnp.zeros((block, features), f32)
    for k in range(z_size):
        pick = iota((block, slots), 0) + first == ids_ref[k : k + 1, :slots]
        pick = jnp.where(pick, 1.0, 0.0).astype(bf16)
        gradient = gradient + jnp.dot(
            pick, coarse_ref[k * slots : (k + 1) * slots, :], preferred_element_type=f32
        )
        gradient = gradient + jnp.dot(
            pick, fine_ref[k * slots : (k + 1) * slots, :], preferred_element_type=f32
        )
    lanes = ms_ref.shape[1]
    groups = block // lanes
    base = pl.program_id(0) * groups

    def columns(ref):
        return jnp.concatenate(
            [to_column(ref[pl.ds(base + g, 1), :], lanes) for g in range(groups)], axis=0
        )

    moment, second = moments(
        gradient, mc_ref[...], vc_ref[...], columns(ms_ref), columns(vs_ref)
    )
    mc, vc, ms, vs = new_codes(moment, second)
    new_ref[...] = table_ref[...] - update_of(moment, second)
    mcn_ref[...] = mc
    vcn_ref[...] = vc
    for g in range(groups):
        msn_ref[pl.ds(base + g, 1), :] = to_row(ms[g * lanes : (g + 1) * lanes], lanes)
        vsn_ref[pl.ds(base + g, 1), :] = to_row(vs[g * lanes : (g + 1) * lanes], lanes)


def replica_kernel(core, sub, *refs):
    both_refs, refs = refs[: len(refs) // 2 - 2], refs[len(refs) // 2 - 2 :]
    rest_refs, (table_ref, out_hbm, buffer, sems) = refs[:-4], refs[-4:]
    dp_size = len(both_refs)
    z_size = sems.shape[0]
    my_dp, my_z, my_core = place_of()
    copies = []
    for kz in range(z_size):
        row = jnp.bitwise_xor(my_z, kz) * CORES + jnp.bitwise_xor(my_core, core)
        base = row * (dp_size * sub)
        for k in range(dp_size):
            owner = pl.multiple_of(jnp.bitwise_xor(my_dp, k) * sub, sub)
            if kz:
                value = read_coded(rest_refs[k], (kz - 1) * (sub + META), sub)
            else:
                value = read_coded(both_refs[k], 0, sub)
            rows = pl.ds(pl.multiple_of(base + owner, sub), sub)
            buffer[kz, pl.ds(owner, sub), :] = table_ref[rows, :] - value
        copies.append(
            pltpu.make_async_copy(
                buffer.at[kz],
                out_hbm.at[pl.ds(pl.multiple_of(base, dp_size * sub), dp_size * sub), :],
                sems.at[kz],
            )
        )
        copies[-1].start()
    for copy in copies:
        copy.wait()


def replica_rest_kernel(core, sub, *refs):
    replica_kernel(core, sub, *refs[:-4], *refs[-3:])


VMEM = pltpu.VMEM


def whole(memory_space=VMEM):
    return pl.BlockSpec(memory_space=memory_space)


def send(x, axis, flip):
    size = lax.axis_size(axis)
    return lax.ppermute(x, axis, [(i, i ^ flip) for i in range(size)])


def kernel(function, mib, **options):
    return pl.pallas_call(
        function, compiler_params=pltpu.CompilerParams(vmem_limit_bytes=mib << 20), **options
    )


def step(
    bag_index,
    pooled_grad,
    touched_ids,
    owner_counts,
    cold_table,
    cold_moment_codes,
    cold_second_codes,
    cold_moment_scales,
    cold_second_scales,
    hot_table,
    hot_moment_codes,
    hot_second_codes,
    hot_moment_scales,
    hot_second_scales,
):
    dp_size = lax.axis_size("dp")
    row_size = lax.axis_size("row")
    z_size = row_size // CORES
    samples, pool = bag_index.shape
    features = pooled_grad.shape[1]
    touch = touched_ids.shape[1]
    owners = owner_counts.shape[1]
    hot_rows = hot_table.shape[0]
    owned = cold_table.shape[0]
    sub = hot_rows // row_size // dp_size
    sources = CORES * dp_size
    slots = sources * CAP
    shape = jax.ShapeDtypeStruct
    width = max(samples, touch, owners)
    ints = kernel(
        pack_kernel,
        4,
        out_shape=shape((pool + 8, width), i16),
        in_specs=[whole(pltpu.HBM)] * 3,
        out_specs=whole(),
        scratch_shapes=[
            VMEM((pool, samples), i32),
            VMEM((1, touch), i32),
            VMEM((1, owners), i32),
            pltpu.SemaphoreType.DMA((3,)),
        ],
    )(bag_index.T, touched_ids, owner_counts)
    dp_range = range(1, dp_size)
    z_range = range(1, z_size)
    ints_list = [ints] + [send(ints, "dp", k) for k in dp_range]
    pooled_list = [pooled_grad] + [send(pooled_grad, "dp", k) for k in dp_range]
    ints_list = ints_list + [send(x, "row", 1) for x in ints_list]
    pooled_list = pooled_list + [send(x, "row", 1) for x in pooled_list]

    cell = CAP * z_size
    tall = z_size * sub + cell
    dims = (sources, z_size, dp_size, touch, owners, sub, pool, samples, features)
    tally, ids, own_pooled = kernel(
        functools.partial(tally_kernel, dims),
        12 + (sources * tall * samples * 2 >> 20),
        out_shape=[
            shape((sources, tall, samples), bf16),
            shape((max(8, z_size), features), f32),
            shape((samples, features), bf16),
        ],
        in_specs=[whole()] * sources + [whole(pltpu.HBM)],
        out_specs=[whole()] * 3,
        scratch_shapes=[pltpu.SemaphoreType.DMA],
    )(*ints_list, pooled_grad)
    pooled_list = [own_pooled] + pooled_list[1:]
    outs = kernel(
        functools.partial(gradient_kernel, (sources, z_size, sub)),
        14 + (sources * (tall + features) * samples * 2 >> 20),
        out_shape=[shape((sub + META, features), i16)] * z_size
        + [shape((slots + META, features), i16)] * z_size,
        in_specs=[whole()] * (sources + 2),
        out_specs=[whole()] * (2 * z_size),
        scratch_shapes=[
            VMEM((z_size * sub, features), f32),
            VMEM((z_size, slots, features), i32),
        ],
    )(*pooled_list, tally, ids)
    hot_parts = [outs[0]] + [send(outs[k], "row", CORES * k) for k in z_range]
    cold_out = outs[z_size:]
    cold_parts = [cold_out[0]] + [send(cold_out[k], "row", CORES * k) for k in z_range]

    hot_state = (
        hot_moment_codes,
        hot_second_codes,
        hot_moment_scales.reshape(dp_size, sub),
        hot_second_scales.reshape(dp_size, sub),
    )
    update, both = kernel(
        functools.partial(hot_kernel, z_size),
        8,
        out_shape=[
            shape((sub + META, features), i16),
            shape((2 * (sub + META), features), i16),
        ],
        in_specs=[whole()] * (z_size + 4),
        out_specs=[whole()] * 2,
    )(*hot_parts, *hot_state)
    column = [send(update, "row", CORES * k) for k in z_range]
    both = [both] + [send(both, "dp", k) for k in dp_range]
    both_core = [send(x, "row", 1) for x in both]
    rest = kernel(
        join_kernel,
        4,
        out_shape=shape(((z_size - 1) * (sub + META), features), i16),
        in_specs=[whole()] * (z_size - 1),
        out_specs=whole(),
    )(*column)
    rest = [rest] + [send(rest, "dp", k) for k in dp_range]
    rest_core = [send(x, "row", 1) for x in rest]

    hot_mc, hot_vc, hot_ms, hot_vs = kernel(
        functools.partial(spread_kernel, dp_size),
        8,
        out_shape=[shape((dp_size * sub, features), bf16)] * 2 + [shape((dp_size, sub), f32)] * 2,
        in_specs=[whole()] * (dp_size + 4),
        out_specs=[whole()] * 4,
    )(*both, *hot_state)

    block = min(256, owned)
    blocks = owned // block
    lanes = min(128, owned)
    by_rows = pl.BlockSpec((block, features), lambda i: (i, 0))
    by_scales = pl.BlockSpec((owned // lanes, lanes), lambda i: (0, 0))
    cold = kernel(
        functools.partial(cold_kernel, z_size),
        16,
        out_shape=[
            shape((owned, features), f32),
            shape((owned, features), bf16),
            shape((owned, features), bf16),
            shape((owned // lanes, lanes), f32),
            shape((owned // lanes, lanes), f32),
        ],
        grid_spec=pltpu.PrefetchScalarGridSpec(
            num_scalar_prefetch=0,
            grid=(blocks,),
            in_specs=[pl.BlockSpec((slots + META, features), lambda i: (0, 0))] * z_size
            + [by_rows] * 3
            + [by_scales] * 2,
            out_specs=[by_rows] * 3 + [by_scales] * 2,
            scratch_shapes=[
                VMEM((z_size * slots, features), bf16),
                VMEM((z_size * slots, features), bf16),
                VMEM((max(z_size, 8), features), i32),
            ],
        ),
    )(
        *cold_parts,
        cold_table,
        cold_moment_codes,
        cold_second_codes,
        cold_moment_scales.reshape(owned // lanes, lanes),
        cold_second_scales.reshape(owned // lanes, lanes),
    )

    table = kernel(
        fetch_kernel,
        4,
        out_shape=shape((hot_rows, features), f32),
        in_specs=[whole(pltpu.HBM)],
        out_specs=whole(),
        scratch_shapes=[pltpu.SemaphoreType.DMA],
    )(hot_table)
    scratch = [
        VMEM((z_size, dp_size * sub, features), f32),
        pltpu.SemaphoreType.DMA((z_size,)),
    ]
    half = kernel(
        functools.partial(replica_kernel, 0, sub),
        8,
        out_shape=shape((hot_rows, features), f32),
        in_specs=[whole()] * (2 * dp_size + 1),
        out_specs=whole(pltpu.HBM),
        scratch_shapes=scratch,
    )(*both, *rest, table)
    replica = kernel(
        functools.partial(replica_rest_kernel, 1, sub),
        8,
        out_shape=shape((hot_rows, features), f32),
        in_specs=[whole()] * (2 * dp_size + 1) + [whole(pltpu.HBM)],
        out_specs=whole(pltpu.HBM),
        scratch_shapes=scratch,
        input_output_aliases={2 * dp_size + 1: 0},
    )(*both_core, *rest_core, table, half)
    return (
        cold[0],
        cold[1],
        cold[2],
        cold[3].reshape(owned),
        cold[4].reshape(owned),
        replica,
        hot_mc,
        hot_vc,
        hot_ms.reshape(dp_size * sub),
        hot_vs.reshape(dp_size * sub),
    )


def solution(mesh):
    return jax.shard_map(
        step,
        mesh=mesh,
        in_specs=(
            P(("dp", "row"), None),
            P(("dp", "row"), None),
            P(("dp", "row"), None),
            P(("dp", "row"), None),
            P(("dp", "row"), None),
            P(("dp", "row"), None),
            P(("dp", "row"), None),
            P(("dp", "row")),
            P(("dp", "row")),
            P(),
            P("row", None),
            P("row", None),
            P("row"),
            P("row"),
        ),
        out_specs=(
            P(("dp", "row"), None),
            P(("dp", "row"), None),
            P(("dp", "row"), None),
            P(("dp", "row")),
            P(("dp", "row")),
            P(),
            P("row", None),
            P("row", None),
            P("row"),
            P("row"),
        ),
        check_vma=False,
    )
```
